32 devices in a mesh: grp: 1, mid: 16 (over z, y, core), off: 2 (over x), sub: 1.
Axes of the slice: x: 2, y: 2, z: 4, core: 2. Of those that a mesh axis runs over, the one named last changes fastest.
Arguments:
- traces: bfloat16 [2, 1024, 1024], P('off', ('grp', 'mid'), 'sub'), may hold values from -6 to 6
- centre_offset: int32 [256], P(('grp', 'mid')), may hold values from 0 to 63
- foot_start: int32 [256, 16], P('grp'), may hold values from 0 to 240
- beam_count: int32 [16], P('grp'), may hold values from 2 to 16, as said below
- operator: bfloat16 [1024, 65536], P('sub', 'mid'), may hold values from -0.1875 to 0.1875
Outputs:
- image: float32 [256, 256], P(('grp', 'mid'))
The draws below stay inside these ranges and needn't reach their ends.
Inputs may be any that keep to these rules, and one draw needn't show every extreme that they name: `beam_count`: the live beams of all tiles sum to exactly 128, and the largest count is exactly 16.
All inputs are finite; a program needn't handle non-finite values.
Results may differ from the reference program's by a relative error of at most 0.0028.
Values may be sent and summed in bfloat16 or wider, within the bound.
A program may use at most 64 MiB of HBM per device.

```python
import math
import jax
import jax.numpy as jnp
from jax import lax

NT = 1024
P_SIZE = 16
FL = 16
DEPTH = 256
HALF = 16
CB_DEV = 16
TR_DEV = 64
CENTRES = 256
TRACES = 1024
TILES = 16
LIVE = 128
OFFSETS = 2
FSUB = 512
FOOT = 4096
N_SUB = 1


def draw_foot_start(key, part):
    centre = jnp.arange(CENTRES, dtype=jnp.int32)[:, None]
    slope_index = jnp.arange(P_SIZE, dtype=jnp.int32)[None, :]
    drift = (2 * slope_index - P_SIZE + 1) * FL // (4 * P_SIZE)
    jitter = jax.random.randint(jax.random.fold_in(key, 7), (CENTRES, P_SIZE), -(FL // 2), FL // 2 + 1)
    return jnp.clip(centre - FL // 2 + drift + jitter, 0, CENTRES - FL).astype(jnp.int32)


def draw_centre_offset(key, part):
    slot = jnp.arange(CENTRES, dtype=jnp.int32) % CB_DEV
    reach = max(1, HALF // 2)
    anywhere = jax.random.randint(jax.random.fold_in(key, 11), (CENTRES,), 0, TR_DEV)
    lower = jax.random.randint(jax.random.fold_in(key, 12), (CENTRES,), 0, reach)
    upper = TR_DEV - 1 - jax.random.randint(jax.random.fold_in(key, 13), (CENTRES,), 0, reach)
    return jnp.where(slot == 0, lower, jnp.where(slot == 1, upper, anywhere)).astype(jnp.int32)


def draw_beam_count(key, part):
    order = jax.random.permutation(jax.random.fold_in(key, 21), TILES).astype(jnp.int32)
    rank = jnp.argsort(order, stable=True).astype(jnp.int32)
    spare = CB_DEV - 2
    remain = LIVE - CB_DEV - 2 * (TILES - 1)
    extra = jnp.clip(remain - (rank - 1) * spare, 0, spare)
    return jnp.where(rank == 0, CB_DEV, 2 + extra).astype(jnp.int32)


def shard_levels(key, extent, cuts, low, high):
    def one(dim, shards_of):
        draws = jax.random.uniform(jax.random.fold_in(jax.random.fold_in(key, 6), dim), (shards_of,), jnp.float32, low / len(cuts), high / len(cuts))
        return jnp.repeat(jnp.exp(draws), extent[dim] // shards_of).reshape((-1,) + (1,) * (len(extent) - dim - 1))

    factor_of = one(*cuts[0])
    for cut in cuts[1:]:
        factor_of = factor_of * one(*cut)
    return factor_of


def centred(rng, dims, deviation, bound, pieces=(), held_as=jnp.bfloat16):
    entries = deviation * jax.random.normal(rng, dims, jnp.float32)
    if pieces:
        entries = entries * shard_levels(rng, dims, pieces, -0.22, 0.18)
    return jnp.clip(entries, -bound, bound).astype(held_as)


def setup_inputs(seed: int = 0, part: int = 0) -> dict:
    streams_of = jax.random.split(jax.random.key(seed), 6)
    own_keys = jax.random.split(jax.random.fold_in(streams_of[5], part), 6)
    traces = centred(own_keys[0], (OFFSETS, TRACES, NT), 1.0, 6.0, ((0, 2), (1, 16)))
    centre_offset = draw_centre_offset(jax.random.fold_in(jax.random.fold_in(streams_of[5], part), 71), part)
    foot_start = draw_foot_start(jax.random.fold_in(jax.random.fold_in(streams_of[5], part), 71), part)
    beam_count = draw_beam_count(jax.random.fold_in(jax.random.fold_in(streams_of[5], part), 71), part)
    operator = centred(streams_of[4], (NT, P_SIZE * FOOT), NT ** -0.5, 0.1875, ((1, 16),))
    return {"traces": traces, "centre_offset": centre_offset, "foot_start": foot_start, "beam_count": beam_count, "operator": operator}


def dft_rows(first_row, row_count, freq_block):
    sample_index = first_row + jnp.arange(row_count, dtype=jnp.int32)[:, None]
    column = jnp.arange(NT, dtype=jnp.int32)[None, :]
    within = column % (2 * freq_block)
    frequency = column // (2 * freq_block) * freq_block + within % freq_block
    phase_angle = 2.0 * math.pi / NT * (sample_index * frequency % NT).astype(jnp.float32)
    values = jnp.where(within // freq_block == 1, -jnp.sin(phase_angle), jnp.cos(phase_angle))
    return values / math.sqrt(NT)

def slant_weights(frequency):
    offsets = jnp.arange(-HALF, HALF + 1, dtype=jnp.int32).astype(jnp.float32)
    taper = jnp.exp(-0.5 * (1.5 * offsets / HALF) ** 2)
    taper = taper / jnp.sqrt(jnp.sum(taper * taper))
    slopes = 0.25 * (jnp.arange(P_SIZE, dtype=jnp.int32).astype(jnp.float32) - 0.5 * (P_SIZE - 1))
    theta = 2.0 * math.pi / NT * slopes[:, None, None] * offsets[None, :, None] * frequency.astype(jnp.float32)[None, None, :]
    return (taper[None, :, None] * jnp.cos(theta), taper[None, :, None] * jnp.sin(theta))

def form_beams(windows_real, windows_imag, cos_weight, sin_weight):
    high = lax.Precision.HIGHEST
    beam_real = jnp.einsum('pxf,bxf->bpf', cos_weight, windows_real, precision=high) + jnp.einsum('pxf,bxf->bpf', sin_weight, windows_imag, precision=high)
    beam_imag = jnp.einsum('pxf,bxf->bpf', cos_weight, windows_imag, precision=high) - jnp.einsum('pxf,bxf->bpf', sin_weight, windows_real, precision=high)
    return (beam_real, beam_imag)

def live_rows(beam_count, per_tile, live_total):
    tile_ends = jnp.cumsum(beam_count).astype(jnp.int32)
    position = jnp.arange(live_total, dtype=jnp.int32)
    owner = lax.optimization_barrier(jnp.sum((position[:, None] >= tile_ends[None, :]).astype(jnp.int32), axis=1))
    first = tile_ends - beam_count.astype(jnp.int32)
    match = owner[:, None] == jnp.arange(beam_count.shape[0], dtype=jnp.int32)[None, :]
    chosen = lax.optimization_barrier(jnp.sum(jnp.where(match, first[None, :], 0), axis=1))
    return (owner * per_tile + position - chosen).astype(jnp.int32)

def reference(traces, centre_offset, foot_start, beam_count, operator):
    high = lax.Precision.HIGHEST
    dft_table = dft_rows(0, NT, FSUB)
    chosen = live_rows(beam_count, CB_DEV, LIVE)
    centre_trace = chosen // CB_DEV * TR_DEV + centre_offset[chosen]
    window_index = (centre_trace[:, None] + jnp.arange(2 * HALF + 1, dtype=jnp.int32)[None, :]).astype(jnp.int32)
    cos_weight, sin_weight = slant_weights(jnp.arange(NT // 2, dtype=jnp.int32))
    beam_sum = jnp.zeros((LIVE, P_SIZE, NT), jnp.float32)
    for offset_class in range(OFFSETS):
        spectra = jnp.dot(traces[offset_class].astype(jnp.float32), dft_table, precision=high)
        shaped = spectra.reshape(TRACES, N_SUB, 2, FSUB)
        real_all = jnp.pad(shaped[:, :, 0, :].reshape(TRACES, NT // 2), ((HALF, HALF), (0, 0)))
        imag_all = jnp.pad(shaped[:, :, 1, :].reshape(TRACES, NT // 2), ((HALF, HALF), (0, 0)))
        beam_real, beam_imag = form_beams(real_all[window_index], imag_all[window_index], cos_weight, sin_weight)
        stacked = jnp.stack([beam_real.reshape(LIVE, P_SIZE, N_SUB, FSUB), beam_imag.reshape(LIVE, P_SIZE, N_SUB, FSUB)], axis=3).reshape(LIVE, P_SIZE, NT)
        rounded = lax.optimization_barrier(stacked.astype(jnp.bfloat16))
        beam_sum = beam_sum + rounded.astype(jnp.float32)
    starts_live = foot_start[chosen]
    image = jnp.zeros((CENTRES, DEPTH), jnp.float32)
    lateral = jnp.arange(FL, dtype=jnp.int32)
    for slope in range(P_SIZE):
        kernel = operator[:, slope * FOOT:(slope + 1) * FOOT].astype(jnp.float32)
        footprint = jnp.dot(beam_sum[:, slope, :], kernel, precision=high)
        target = (starts_live[:, slope][:, None] + lateral[None, :]).reshape(-1)
        image = image.at[target].add(footprint.reshape(LIVE * FL, DEPTH))
    return image / math.sqrt(FL * P_SIZE)
```

```python
import functools
import math

import jax
import jax.numpy as jnp
import numpy as np
from jax import lax
from jax.experimental import pallas as pl
from jax.experimental.pallas import tpu as pltpu
from jax.sharding import PartitionSpec as P

P_SIZE = 16
FL = 16
DEPTH = 256
HALF = 16
LANES = 128
F32 = jnp.float32
BF16 = jnp.bfloat16


def dft_quarter(total, parts):
    block = total // 2 // parts
    frequency = np.arange(total // 2)
    phase = 2.0 * np.pi / total * (np.arange(total // 4)[:, None] * frequency[None, :] % total)
    pair = np.stack([np.cos(phase), -np.sin(phase)]) / math.sqrt(total)
    pair = pair.reshape(2, total // 4, parts, block // LANES, LANES)
    table = pair.transpose(2, 1, 3, 0, 4).reshape(parts, total // 4, 2 * block).astype(np.float32)
    high = table.astype(BF16)
    low = (table - high.astype(np.float32)).astype(BF16)
    return high, low


def half_weights(total, parts):
    offsets = np.arange(-HALF, HALF + 1)
    taper = np.exp(-0.5 * (1.5 * offsets / HALF) ** 2)
    taper = (taper / np.sqrt(np.sum(taper * taper)))[HALF:]
    slopes = 0.25 * (np.arange(P_SIZE // 2, P_SIZE) - 0.5 * (P_SIZE - 1))
    theta = (
        2.0 * np.pi / total
        * np.arange(HALF + 1)[:, None, None] * slopes[None, :, None]
        * np.arange(total // 2)[None, None, :]
    )
    both = np.stack([np.cos(theta), np.sin(theta)]) * taper[None, :, None, None]
    both = both.reshape(2, HALF + 1, P_SIZE // 2, parts, -1).transpose(3, 0, 1, 2, 4)
    return both.astype(np.float32)


def kernel(
    sizes,
    traces_ref, offset_ref, start_ref, count_ref, operator_ref, high_ref, low_ref, weight_ref,
    out_ref,
    ext, high, low, weight, oper, spec, stage, send, recv, gathered, image, parts, tile, peers,
    load_sem, halo_send, halo_recv, beam_send, beam_recv, part_send, part_recv, peer_send, peer_recv,
):
    mids, offs, subs = sizes
    rep = mids // P_SIZE
    me = lax.axis_index("mid")
    group = offs * subs
    mine = lax.axis_index("off") * subs + lax.axis_index("sub")
    rows = traces_ref.shape[0]
    total = traces_ref.shape[1]
    quarter = total // 4
    samples = operator_ref.shape[0]
    block = samples // 2
    chunks = block // LANES
    beams = offset_ref.shape[0]
    laterals = operator_ref.shape[1] // DEPTH
    first_freq = lax.axis_index("sub") * block

    def member(k):
        other = lax.rem(mine + k, group)
        return other, {"off": other // subs, "sub": lax.rem(other, subs)}

    load_ext = pltpu.make_async_copy(traces_ref, ext.at[pl.ds(HALF, rows)], load_sem.at[0])
    load_high = pltpu.make_async_copy(high_ref, high, load_sem.at[1])
    load_low = pltpu.make_async_copy(low_ref, low, load_sem.at[2])
    load_weight = pltpu.make_async_copy(weight_ref, weight, load_sem.at[3])
    load_oper = pltpu.make_async_copy(operator_ref, oper, load_sem.at[4])
    load_ext.start()
    load_high.start()
    load_low.start()
    load_weight.start()
    load_oper.start()

    barrier = pltpu.get_barrier_semaphore()

    @pl.loop(1, mids)
    def _(k):
        pl.semaphore_signal(barrier, inc=1, device_id={"mid": lax.rem(me + k, mids)})

    @pl.loop(1, group)
    def _(k):
        pl.semaphore_signal(barrier, inc=1, device_id=member(k)[1])

    pl.semaphore_wait(barrier, mids - 1 + group - 1)

    right, left = lax.rem(me + 1, mids), lax.rem(me + mids - 1, mids)
    to_right = pltpu.make_async_remote_copy(
        traces_ref.at[pl.ds(rows - HALF, HALF)], ext.at[pl.ds(0, HALF)],
        halo_send.at[0], halo_recv.at[0], device_id={"mid": right},
    )
    to_left = pltpu.make_async_remote_copy(
        traces_ref.at[pl.ds(0, HALF)], ext.at[pl.ds(HALF + rows, HALF)],
        halo_send.at[1], halo_recv.at[1], device_id={"mid": left},
    )
    to_right.start()
    to_left.start()

    centres = start_ref.shape[0]
    slope = me // rep
    lateral_first = lax.rem(me, rep) * laterals
    lane = lax.broadcasted_iota(jnp.int32, start_ref.shape, 1)
    starts = jnp.sum(jnp.where(lane == slope, start_ref[...], 0), axis=1, keepdims=True)
    beam_id = lax.broadcasted_iota(jnp.int32, (centres, mids), 0)
    tile_id = lax.broadcasted_iota(jnp.int32, (centres, mids), 1)
    slot = beam_id - tile_id * beams
    alive = (slot >= 0) & (slot < count_ref[...])
    alive = jnp.sum(jnp.where(alive, 1, 0), axis=1, keepdims=True)
    target = jnp.where(alive > 0, starts + lateral_first, -1)
    hot = (target == lax.broadcasted_iota(jnp.int32, (centres, centres), 1)).astype(F32)
    hot = hot.T.astype(BF16)

    load_ext.wait()
    load_high.wait()
    load_low.wait()
    to_right.wait()
    to_left.wait()

    inside_low = (me > 0).astype(F32)
    inside_high = (me < mids - 1).astype(F32)
    row = lax.broadcasted_iota(jnp.int32, (rows + 2 * HALF, LANES), 0)
    keep = jnp.where(row < HALF, inside_low, jnp.where(row >= HALF + rows, inside_high, 1.0))
    stacked = jnp.concatenate([ext[:, q * quarter:(q + 1) * quarter] for q in range(4)], axis=0)
    count = rows + 2 * HALF
    for c in range(chunks):
        wide = slice(2 * c * LANES, 2 * (c + 1) * LANES)
        y = jnp.dot(stacked, high[:, wide], preferred_element_type=F32)
        y = y + jnp.dot(stacked, low[:, wide], preferred_element_type=F32)
        y0, y1, y2, y3 = (y[q * count:(q + 1) * count] for q in range(4))
        even_sum, even_dif, odd_sum, odd_dif = y0 + y2, y0 - y2, y1 + y3, y1 - y3
        f = first_freq + c * LANES + lax.broadcasted_iota(jnp.int32, (count, LANES), 1)
        phase = lax.rem(f, 4)
        sign = jnp.where(phase < 2, 1.0, -1.0)
        odd = lax.rem(f, 2) == 1
        real = jnp.where(
            odd, even_dif[:, :LANES] + sign * odd_dif[:, LANES:],
            even_sum[:, :LANES] + sign * odd_sum[:, :LANES],
        ) * keep
        imag = jnp.where(
            odd, even_dif[:, LANES:] - sign * odd_dif[:, :LANES],
            even_sum[:, LANES:] + sign * odd_sum[:, LANES:],
        ) * keep
        pairs = P_SIZE // 2
        spec[:, :, c * LANES:(c + 1) * LANES] = jnp.broadcast_to(
            real[:, None, :], (count, pairs, LANES))
        spec[:, :, block + c * LANES:block + (c + 1) * LANES] = jnp.broadcast_to(
            imag[:, None, :], (count, pairs, LANES))

    load_weight.wait()
    pairs = P_SIZE // 2

    @pl.loop(0, beams)
    def _(b):
        centre = offset_ref[b] + HALF
        for c in range(chunks):
            re = slice(c * LANES, (c + 1) * LANES)
            im = slice(block + c * LANES, block + (c + 1) * LANES)
            cos0 = weight[0, 0, :, re]
            a_re = cos0 * spec[centre, :, re]
            a_im = cos0 * spec[centre, :, im]
            b_re = jnp.zeros_like(a_re)
            b_im = jnp.zeros_like(a_re)
            for x in range(1, HALF + 1):
                r_up, r_dn = spec[centre + x, :, re], spec[centre - x, :, re]
                i_up, i_dn = spec[centre + x, :, im], spec[centre - x, :, im]
                cos, sin = weight[0, x, :, re], weight[1, x, :, re]
                a_re += cos * (r_up + r_dn)
                a_im += cos * (i_up + i_dn)
                b_re += sin * (i_up - i_dn)
                b_im += sin * (r_up - r_dn)
            at = pl.ds(pl.multiple_of(b * pairs, pairs), pairs)
            stage[c, 0, at, :] = a_re + b_re
            stage[c, 1, at, :] = a_im - b_im
            stage[c, 2, at, :] = a_re - b_re
            stage[c, 3, at, :] = a_im + b_im

    for p in range(pairs):
        for c in range(chunks):
            for part in range(2):
                lanes = slice(part * block + c * LANES, part * block + (c + 1) * LANES)
                every = pl.ds(p, beams, stride=pairs)
                send[pairs + p, :, lanes] = stage.at[c, part][every, :].astype(BF16)
                send[pairs - 1 - p, :, lanes] = stage.at[c, 2 + part][every, :].astype(BF16)

    def beam_copy(k, to, source):
        return pltpu.make_async_remote_copy(
            send.at[to // rep], recv.at[pl.ds(pl.multiple_of(source * beams, beams), beams)],
            beam_send.at[k], beam_recv.at[source], device_id={"mid": to},
        )

    @pl.loop(1, mids)
    def _(k):
        beam_copy(k, lax.rem(me + k, mids), me).start()

    recv[pl.ds(pl.multiple_of(me * beams, beams), beams), :] = send[slope]

    @pl.loop(1, mids)
    def _(k):
        beam_copy(k, lax.rem(me + k, mids), lax.rem(me + mids - k, mids)).wait()

    gathered[...] = jnp.dot(hot, recv[...], preferred_element_type=F32).astype(BF16)
    load_oper.wait()
    image[...] = jnp.zeros_like(image)

    @pl.loop(0, laterals)
    def _(step):
        l = laterals - 1 - step
        columns = pl.ds(pl.multiple_of(l * DEPTH, DEPTH), DEPTH)
        foot = jnp.dot(gathered[...], oper[:, columns], preferred_element_type=F32)
        image[...] = pltpu.roll(image[...], 1, 0) + foot

    def part_copy(k, to, source):
        return pltpu.make_async_remote_copy(
            image.at[pl.ds(pl.multiple_of(to * beams, beams), beams)], parts.at[source],
            part_send.at[k], part_recv.at[source], device_id={"mid": to},
        )

    @pl.loop(1, mids)
    def _(k):
        part_copy(k, lax.rem(me + k, mids), me).start()

    parts[me] = image[pl.ds(pl.multiple_of(me * beams, beams), beams), :]

    @pl.loop(1, mids)
    def _(k):
        part_copy(k, lax.rem(me + k, mids), lax.rem(me + mids - k, mids)).wait()

    tile[...] = jnp.sum(parts[...], axis=0) * (1.0 / math.sqrt(FL * P_SIZE))

    def peer_copy(k, to, source):
        return pltpu.make_async_remote_copy(
            tile, peers.at[source], peer_send.at[k], peer_recv.at[source], device_id=to,
        )

    @pl.loop(1, group)
    def _(k):
        peer_copy(k, member(k)[1], mine).start()

    peers[mine] = tile[...]

    @pl.loop(1, group)
    def _(k):
        peer_copy(k, member(k)[1], lax.rem(mine + group - k, group)).wait()

    out_ref[...] = jnp.sum(peers[...], axis=0)


def shards(traces, centre_offset, foot_start, beam_count, operator):
    mids, offs, subs = (lax.axis_size(name) for name in ("mid", "off", "sub"))
    traces = traces[0]
    if subs > 1:
        traces = lax.all_gather(traces, "sub", axis=1, tiled=True)
    rows, total = traces.shape
    samples, columns = operator.shape
    beams = centre_offset.shape[0]
    centres = foot_start.shape[0]
    group = offs * subs
    high, low = dft_quarter(total, subs)
    weight = half_weights(total, subs)
    pick = (lambda table: table[0]) if subs == 1 else (
        lambda table: lax.dynamic_index_in_dim(jnp.asarray(table), lax.axis_index("sub"), 0, False))
    high, low, weight = (jnp.asarray(pick(table)) for table in (high, low, weight))
    vmem = pl.BlockSpec(memory_space=pltpu.VMEM)
    smem = pl.BlockSpec(memory_space=pltpu.SMEM)
    hbm = pl.BlockSpec(memory_space=pl.ANY)
    dma = pltpu.SemaphoreType.DMA
    chunks = samples // 2 // LANES
    return pl.pallas_call(
        functools.partial(kernel, (mids, offs, subs)),
        out_shape=jax.ShapeDtypeStruct((beams, DEPTH), F32),
        in_specs=[hbm, smem, vmem, vmem, hbm, hbm, hbm, hbm],
        out_specs=vmem,
        scratch_shapes=[
            pltpu.VMEM((rows + 2 * HALF, total), BF16),
            pltpu.VMEM(high.shape, BF16),
            pltpu.VMEM(low.shape, BF16),
            pltpu.VMEM(weight.shape, F32),
            pltpu.VMEM((samples, columns), BF16),
            pltpu.VMEM((rows + 2 * HALF, P_SIZE // 2, samples), F32),
            pltpu.VMEM((chunks, 4, beams * P_SIZE // 2, LANES), F32),
            pltpu.VMEM((P_SIZE, beams, samples), BF16),
            pltpu.VMEM((mids * beams, samples), BF16),
            pltpu.VMEM((centres, samples), BF16),
            pltpu.VMEM((centres, DEPTH), F32),
            pltpu.VMEM((mids, beams, DEPTH), F32),
            pltpu.VMEM((beams, DEPTH), F32),
            pltpu.VMEM((group, beams, DEPTH), F32),
            dma((5,)),
            dma((2,)),
            dma((2,)),
            dma((mids,)),
            dma((mids,)),
            dma((mids,)),
            dma((mids,)),
            dma((group,)),
            dma((group,)),
        ],
        compiler_params=pltpu.CompilerParams(
            collective_id=0, has_side_effects=True, vmem_limit_bytes=48 * 1024 * 1024),
    )(traces, centre_offset, foot_start, beam_count.reshape(1, -1), operator, high, low, weight)


def solution(mesh):
    return jax.shard_map(
        shards,
        mesh=mesh,
        in_specs=(
            P("off", ("grp", "mid"), "sub"),
            P(("grp", "mid")),
            P("grp", None),
            P("grp"),
            P("sub", "mid"),
        ),
        out_specs=P(("grp", "mid"), None),
        check_vma=False,
    )
```

```python
import functools
import math

import jax
import jax.numpy as jnp
import numpy as np
from jax import lax
from jax.experimental import pallas as pl
from jax.experimental.pallas import tpu as pltpu
from jax.sharding import PartitionSpec as P

P_SIZE = 16
FL = 16
DEPTH = 256
HALF = 16
LANES = 128
F32 = jnp.float32
BF16 = jnp.bfloat16


def dft_quarter(total, parts):
    block = total // 2 // parts
    frequency = np.arange(total // 2)
    phase = 2.0 * np.pi / total * (np.arange(total // 4)[:, None] * frequency[None, :] % total)
    pair = np.stack([np.cos(phase), -np.sin(phase)]) / math.sqrt(total)
    pair = pair.reshape(2, total // 4, parts, block // LANES, LANES)
    table = pair.transpose(2, 1, 3, 0, 4).reshape(parts, total // 4, 2 * block).astype(np.float32)
    high = table.astype(BF16)
    low = (table - high.astype(np.float32)).astype(BF16)
    return high, low


def half_weights(total, parts):
    offsets = np.arange(-HALF, HALF + 1)
    taper = np.exp(-0.5 * (1.5 * offsets / HALF) ** 2)
    taper = (taper / np.sqrt(np.sum(taper * taper)))[HALF:]
    slopes = 0.25 * (np.arange(P_SIZE // 2, P_SIZE) - 0.5 * (P_SIZE - 1))
    theta = (
        2.0 * np.pi / total
        * np.arange(HALF + 1)[:, None, None] * slopes[None, :, None]
        * np.arange(total // 2)[None, None, :]
    )
    both = np.stack([np.cos(theta), np.sin(theta)]) * taper[None, :, None, None]
    both = both.reshape(2, HALF + 1, P_SIZE // 2, parts, -1).transpose(3, 0, 1, 2, 4)
    return both.astype(np.float32)


def kernel(
    sizes,
    traces_ref, offset_ref, start_ref, count_ref, operator_ref, high_ref, low_ref, weight_ref,
    out_ref,
    ext, high, low, weight, oper, spec, stage, send, recv, image, outgoing, parts, tile, peers,
    load_sem, oper_sem, halo_send, halo_recv, beam_send, beam_recv, part_send, part_recv,
    peer_send, peer_recv,
):
    mids, offs, subs = sizes
    rep = mids // P_SIZE
    me = lax.axis_index("mid")
    group = offs * subs
    mine = lax.axis_index("off") * subs + lax.axis_index("sub")
    rows = traces_ref.shape[0]
    total = traces_ref.shape[1]
    quarter = total // 4
    samples = operator_ref.shape[0]
    block = samples // 2
    chunks = block // LANES
    beams = offset_ref.shape[0]
    pairs = P_SIZE // 2
    laterals = operator_ref.shape[1] // DEPTH
    first_freq = lax.axis_index("sub") * block

    def member(k):
        other = lax.rem(mine + k, group)
        return other, {"off": other // subs, "sub": lax.rem(other, subs)}

    barrier = pltpu.get_barrier_semaphore()

    @pl.loop(1, mids)
    def _(k):
        pl.semaphore_signal(barrier, inc=1, device_id={"mid": lax.rem(me + k, mids)})

    @pl.loop(1, group)
    def _(k):
        pl.semaphore_signal(barrier, inc=1, device_id=member(k)[1])

    load_ext = pltpu.make_async_copy(traces_ref, ext.at[pl.ds(HALF, rows)], load_sem.at[0])
    load_high = pltpu.make_async_copy(high_ref, high, load_sem.at[1])
    load_low = pltpu.make_async_copy(low_ref, low, load_sem.at[2])
    load_weight = pltpu.make_async_copy(weight_ref, weight, load_sem.at[3])
    load_oper = [
        pltpu.make_async_copy(
            operator_ref.at[pl.ds(part * block + c * LANES, LANES)],
            oper.at[c, pl.ds(part * LANES, LANES)], oper_sem.at[c, part],
        )
        for c in range(chunks) for part in range(2)
    ]
    for load in (load_ext, load_high, load_low, load_weight, *load_oper):
        load.start()

    centres = start_ref.shape[1]
    slope = me // rep
    lateral_first = lax.rem(me, rep) * laterals
    at_slope = lax.broadcasted_iota(jnp.int32, start_ref.shape, 0) == slope
    starts = jnp.sum(jnp.where(at_slope, start_ref[...], 0), axis=0, keepdims=True)
    beam_id = lax.broadcasted_iota(jnp.int32, (1, centres), 1)
    counts = jnp.zeros((1, centres), jnp.int32)
    for t in range(mids):
        inside = (beam_id >= t * beams) & (beam_id < (t + 1) * beams)
        counts = jnp.where(inside, count_ref[t] + t * beams, counts)
    target = jnp.where(beam_id < counts, starts + lateral_first, -1)
    hot = (target == lax.broadcasted_iota(jnp.int32, (centres, centres), 0)).astype(F32)
    hot = hot.astype(BF16)

    pl.semaphore_wait(barrier, mids - 1 + group - 1)

    right, left = lax.rem(me + 1, mids), lax.rem(me + mids - 1, mids)
    to_right = pltpu.make_async_remote_copy(
        traces_ref.at[pl.ds(rows - HALF, HALF)], ext.at[pl.ds(0, HALF)],
        halo_send.at[0], halo_recv.at[0], device_id={"mid": right},
    )
    to_left = pltpu.make_async_remote_copy(
        traces_ref.at[pl.ds(0, HALF)], ext.at[pl.ds(HALF + rows, HALF)],
        halo_send.at[1], halo_recv.at[1], device_id={"mid": left},
    )
    to_right.start()
    to_left.start()

    def transform(c, pieces, keep, ranges):
        wide = slice(2 * c * LANES, 2 * (c + 1) * LANES)
        y = jnp.dot(pieces, high[:, wide], preferred_element_type=F32)
        y = y + jnp.dot(pieces, low[:, wide], preferred_element_type=F32)
        count = pieces.shape[0] // 4
        y0, y1, y2, y3 = (y[q * count:(q + 1) * count] for q in range(4))
        even_sum, even_dif, odd_sum, odd_dif = y0 + y2, y0 - y2, y1 + y3, y1 - y3
        f = first_freq + c * LANES + lax.broadcasted_iota(jnp.int32, (count, LANES), 1)
        sign = jnp.where(lax.rem(f, 4) < 2, 1.0, -1.0)
        odd = lax.rem(f, 2) == 1
        real = jnp.where(
            odd, even_dif[:, :LANES] + sign * odd_dif[:, LANES:],
            even_sum[:, :LANES] + sign * odd_sum[:, :LANES],
        ) * keep
        imag = jnp.where(
            odd, even_dif[:, LANES:] - sign * odd_dif[:, :LANES],
            even_sum[:, LANES:] + sign * odd_sum[:, LANES:],
        ) * keep
        for first, at, size in ranges:
            for part, value in enumerate((real, imag)):
                spec[c, part, at:at + size] = jnp.broadcast_to(
                    value[first:first + size, None, :], (size, pairs, LANES))

    load_ext.wait()
    load_high.wait()
    load_low.wait()
    own = jnp.concatenate(
        [ext[HALF:HALF + rows, q * quarter:(q + 1) * quarter] for q in range(4)], axis=0)
    for c in range(chunks):
        transform(c, own, 1.0, [(0, HALF, rows)])

    load_weight.wait()
    to_right.wait()
    to_left.wait()
    sides = [slice(0, HALF), slice(HALF + rows, 2 * HALF + rows)]
    edge = jnp.concatenate(
        [ext[side, q * quarter:(q + 1) * quarter] for q in range(4) for side in sides], axis=0)
    row = lax.broadcasted_iota(jnp.int32, (2 * HALF, LANES), 0)
    keep = jnp.where(row < HALF, (me > 0).astype(F32), (me < mids - 1).astype(F32))

    def beam_copy(c, k, to, source):
        return pltpu.make_async_remote_copy(
            send.at[c, to // rep],
            recv.at[c, pl.ds(pl.multiple_of(source * beams, beams), beams)],
            beam_send.at[c, k], beam_recv.at[c, source], device_id={"mid": to},
        )

    for c in range(chunks):
        transform(c, edge, keep, [(0, 0, HALF), (HALF, HALF + rows, HALF)])
        re = slice(c * LANES, (c + 1) * LANES)

        @pl.loop(0, beams)
        def _(b):
            centre = offset_ref[b] + HALF
            cos0 = weight[0, 0, :, re]
            a_re = cos0 * spec[c, 0, centre]
            a_im = cos0 * spec[c, 1, centre]
            b_re = jnp.zeros_like(a_re)
            b_im = jnp.zeros_like(a_re)
            for x in range(1, HALF + 1):
                r_up, r_dn = spec[c, 0, centre + x], spec[c, 0, centre - x]
                i_up, i_dn = spec[c, 1, centre + x], spec[c, 1, centre - x]
                cos, sin = weight[0, x, :, re], weight[1, x, :, re]
                a_re += cos * (r_up + r_dn)
                a_im += cos * (i_up + i_dn)
                b_re += sin * (i_up - i_dn)
                b_im += sin * (r_up - r_dn)
            at = pl.ds(pl.multiple_of(b * pairs, pairs), pairs)
            stage[c, 0, at, :] = a_re + b_re
            stage[c, 1, at, :] = a_im - b_im
            stage[c, 2, at, :] = a_re - b_re
            stage[c, 3, at, :] = a_im + b_im

        for p in range(pairs):
            for part in range(2):
                lanes = slice(part * LANES, (part + 1) * LANES)
                every = pl.ds(p, beams, stride=pairs)
                send[c, pairs + p, :, lanes] = stage.at[c, part][every, :].astype(BF16)
                send[c, pairs - 1 - p, :, lanes] = stage.at[c, 2 + part][every, :].astype(BF16)

        @pl.loop(0, mids - 1)
        def _(i):
            k = lax.rem(i + mids // 2, mids)
            k = jnp.where(i + mids // 2 >= mids, k + 1, k)
            beam_copy(c, k, lax.rem(me + k, mids), me).start()

        recv[c, pl.ds(pl.multiple_of(me * beams, beams), beams), :] = send[c, slope]

    for load in load_oper:
        load.wait()

    for c in range(chunks):
        @pl.loop(1, mids)
        def _(k):
            beam_copy(c, k, lax.rem(me + k, mids), lax.rem(me + mids - k, mids)).wait()

        gathered = jnp.dot(hot, recv[c], preferred_element_type=F32).astype(BF16)
        held = jnp.zeros((centres, DEPTH), F32)
        for l in reversed(range(laterals)):
            foot = jnp.dot(
                gathered, oper[c, :, l * DEPTH:(l + 1) * DEPTH], preferred_element_type=F32)
            held = foot if l == laterals - 1 else pltpu.roll(held, 1, 0) + foot
        image[...] = held if c == 0 else image[...] + held

    outgoing[...] = image[...].astype(BF16)

    def part_copy(k, to, source):
        return pltpu.make_async_remote_copy(
            outgoing.at[pl.ds(pl.multiple_of(to * beams, beams), beams)], parts.at[source],
            part_send.at[k], part_recv.at[source], device_id={"mid": to},
        )

    @pl.loop(1, mids)
    def _(k):
        part_copy(k, lax.rem(me + k, mids), me).start()

    home = pl.ds(pl.multiple_of(me * beams, beams), beams)
    parts[me] = outgoing[home, :]

    @pl.loop(1, mids)
    def _(k):
        part_copy(k, lax.rem(me + k, mids), lax.rem(me + mids - k, mids)).wait()

    tile[...] = jnp.sum(parts[...].astype(F32), axis=0) * (1.0 / math.sqrt(FL * P_SIZE))

    def peer_copy(k, to, source):
        return pltpu.make_async_remote_copy(
            tile, peers.at[source], peer_send.at[k], peer_recv.at[source], device_id=to,
        )

    @pl.loop(1, group)
    def _(k):
        peer_copy(k, member(k)[1], mine).start()

    peers[mine] = tile[...]

    @pl.loop(1, group)
    def _(k):
        peer_copy(k, member(k)[1], lax.rem(mine + group - k, group)).wait()

    out_ref[...] = jnp.sum(peers[...], axis=0)


def shards(traces, centre_offset, foot_start, beam_count, operator):
    mids, offs, subs = (lax.axis_size(name) for name in ("mid", "off", "sub"))
    traces = traces[0]
    if subs > 1:
        traces = lax.all_gather(traces, "sub", axis=1, tiled=True)
    rows, total = traces.shape
    samples, columns = operator.shape
    beams = centre_offset.shape[0]
    centres = foot_start.shape[0]
    group = offs * subs
    high, low = dft_quarter(total, subs)
    weight = half_weights(total, subs)
    pick = (lambda table: table[0]) if subs == 1 else (
        lambda table: lax.dynamic_index_in_dim(jnp.asarray(table), lax.axis_index("sub"), 0, False))
    high, low, weight = (jnp.asarray(pick(table)) for table in (high, low, weight))
    vmem = pl.BlockSpec(memory_space=pltpu.VMEM)
    smem = pl.BlockSpec(memory_space=pltpu.SMEM)
    hbm = pl.BlockSpec(memory_space=pl.ANY)
    dma = pltpu.SemaphoreType.DMA
    chunks = samples // 2 // LANES
    return pl.pallas_call(
        functools.partial(kernel, (mids, offs, subs)),
        out_shape=jax.ShapeDtypeStruct((beams, DEPTH), F32),
        in_specs=[hbm, smem, vmem, smem, hbm, hbm, hbm, hbm],
        out_specs=vmem,
        scratch_shapes=[
            pltpu.VMEM((rows + 2 * HALF, total), BF16),
            pltpu.VMEM(high.shape, BF16),
            pltpu.VMEM(low.shape, BF16),
            pltpu.VMEM(weight.shape, F32),
            pltpu.VMEM((chunks, 2 * LANES, columns), BF16),
            pltpu.VMEM((chunks, 2, rows + 2 * HALF, P_SIZE // 2, LANES), F32),
            pltpu.VMEM((chunks, 4, beams * P_SIZE // 2, LANES), F32),
            pltpu.VMEM((chunks, P_SIZE, beams, 2 * LANES), BF16),
            pltpu.VMEM((chunks, mids * beams, 2 * LANES), BF16),
            pltpu.VMEM((centres, DEPTH), F32),
            pltpu.VMEM((centres, DEPTH), BF16),
            pltpu.VMEM((mids, beams, DEPTH), BF16),
            pltpu.VMEM((beams, DEPTH), F32),
            pltpu.VMEM((group, beams, DEPTH), F32),
            dma((4,)),
            dma((chunks, 2)),
            dma((2,)),
            dma((2,)),
            dma((chunks, mids)),
            dma((chunks, mids)),
            dma((mids,)),
            dma((mids,)),
            dma((group,)),
            dma((group,)),
        ],
        compiler_params=pltpu.CompilerParams(
            collective_id=0, has_side_effects=True, vmem_limit_bytes=67043328),
    )(traces, centre_offset, foot_start.T, beam_count, operator, high, low, weight)


def solution(mesh):
    return jax.shard_map(
        shards,
        mesh=mesh,
        in_specs=(
            P("off", ("grp", "mid"), "sub"),
            P(("grp", "mid")),
            P("grp", None),
            P("grp"),
            P("sub", "mid"),
        ),
        out_specs=P(("grp", "mid"), None),
        check_vma=False,
    )
```

```python
import functools
import math

import jax
import jax.numpy as jnp
import numpy as np
from jax import lax
from jax.experimental import pallas as pl
from jax.experimental.pallas import tpu as pltpu
from jax.sharding import PartitionSpec as P

P_SIZE = 16
FL = 16
DEPTH = 256
HALF = 16
LANES = 128
F32 = jnp.float32
BF16 = jnp.bfloat16


def dft_quarter(total, parts):
    block = total // 2 // parts
    frequency = np.arange(total // 2)
    phase = 2.0 * np.pi / total * (np.arange(total // 4)[:, None] * frequency[None, :] % total)
    pair = np.stack([np.cos(phase), -np.sin(phase)]) / math.sqrt(total)
    pair = pair.reshape(2, total // 4, parts, block // LANES, LANES)
    table = pair.transpose(2, 1, 3, 0, 4).reshape(parts, total // 4, 2 * block).astype(np.float32)
    high = table.astype(BF16)
    low = (table - high.astype(np.float32)).astype(BF16)
    return high, low


def half_weights(total, parts):
    offsets = np.arange(-HALF, HALF + 1)
    taper = np.exp(-0.5 * (1.5 * offsets / HALF) ** 2)
    taper = (taper / np.sqrt(np.sum(taper * taper)))[HALF:]
    slopes = 0.25 * (np.arange(P_SIZE // 2, P_SIZE) - 0.5 * (P_SIZE - 1))
    theta = (
        2.0 * np.pi / total
        * np.arange(HALF + 1)[:, None, None] * slopes[None, :, None]
        * np.arange(total // 2)[None, None, :]
    )
    both = np.stack([np.cos(theta), np.sin(theta)]) * taper[None, :, None, None]
    both = both.reshape(2, HALF + 1, P_SIZE // 2, parts, -1).transpose(3, 0, 1, 2, 4)
    return both.astype(np.float32)


def kernel(
    sizes,
    traces_ref, offset_ref, start_ref, count_ref, operator_ref, high_ref, low_ref, weight_ref,
    peers,
    ext, high, low, weight, oper, spec, stage, send, recv, image, outgoing, parts, tile,
    load_sem, oper_sem, halo_send, halo_recv, beam_send, beam_recv, part_send, part_recv,
    peer_send, peer_recv,
):
    mids, offs, subs = sizes
    rep = mids // P_SIZE
    me = lax.axis_index("mid")
    group = offs * subs
    mine = lax.axis_index("off") * subs + lax.axis_index("sub")
    rows = traces_ref.shape[0]
    total = traces_ref.shape[1]
    quarter = total // 4
    samples = operator_ref.shape[0]
    block = samples // 2
    chunks = block // LANES
    beams = offset_ref.shape[0]
    pairs = P_SIZE // 2
    laterals = operator_ref.shape[1] // DEPTH
    centres = start_ref.shape[1]
    slope = me // rep
    first_freq = lax.axis_index("sub") * block

    def member(k):
        other = lax.rem(mine + k, group)
        return other, {"off": other // subs, "sub": lax.rem(other, subs)}

    barrier = pltpu.get_barrier_semaphore()

    @pl.loop(1, mids)
    def _(k):
        pl.semaphore_signal(barrier, inc=1, device_id={"mid": lax.rem(me + k, mids)})

    @pl.loop(1, group)
    def _(k):
        pl.semaphore_signal(barrier, inc=1, device_id=member(k)[1])

    load_ext = pltpu.make_async_copy(traces_ref, ext.at[pl.ds(HALF, rows)], load_sem.at[0])
    load_high = pltpu.make_async_copy(high_ref, high, load_sem.at[1])
    load_low = pltpu.make_async_copy(low_ref, low, load_sem.at[2])
    load_weight = pltpu.make_async_copy(weight_ref, weight, load_sem.at[3])
    load_oper = [
        pltpu.make_async_copy(
            operator_ref.at[pl.ds(part * block + c * LANES, LANES)],
            oper.at[c, pl.ds(part * LANES, LANES)], oper_sem.at[c, part],
        )
        for c in range(chunks) for part in range(2)
    ]
    for load in (load_ext, load_high, load_low, load_weight, *load_oper):
        load.start()

    pl.semaphore_wait(barrier, mids - 1 + group - 1)

    right, left = lax.rem(me + 1, mids), lax.rem(me + mids - 1, mids)
    to_right = pltpu.make_async_remote_copy(
        traces_ref.at[pl.ds(rows - HALF, HALF)], ext.at[pl.ds(0, HALF)],
        halo_send.at[0], halo_recv.at[0], device_id={"mid": right},
    )
    to_left = pltpu.make_async_remote_copy(
        traces_ref.at[pl.ds(0, HALF)], ext.at[pl.ds(HALF + rows, HALF)],
        halo_send.at[1], halo_recv.at[1], device_id={"mid": left},
    )
    to_right.start()
    to_left.start()

    def transform(c, pieces, keep, ranges):
        wide = slice(2 * c * LANES, 2 * (c + 1) * LANES)
        y = jnp.dot(pieces, high[:, wide], preferred_element_type=F32)
        y = y + jnp.dot(pieces, low[:, wide], preferred_element_type=F32)
        count = pieces.shape[0] // 4
        y0, y1, y2, y3 = (y[q * count:(q + 1) * count] for q in range(4))
        even_sum, even_dif, odd_sum, odd_dif = y0 + y2, y0 - y2, y1 + y3, y1 - y3
        f = first_freq + c * LANES + lax.broadcasted_iota(jnp.int32, (count, LANES), 1)
        sign = jnp.where(lax.rem(f, 4) < 2, 1.0, -1.0)
        odd = lax.rem(f, 2) == 1
        real = jnp.where(
            odd, even_dif[:, :LANES] + sign * odd_dif[:, LANES:],
            even_sum[:, :LANES] + sign * odd_sum[:, :LANES],
        ) * keep
        imag = jnp.where(
            odd, even_dif[:, LANES:] - sign * odd_dif[:, :LANES],
            even_sum[:, LANES:] + sign * odd_sum[:, LANES:],
        ) * keep
        for first, at, size in ranges:
            for part, value in enumerate((real, imag)):
                spec[c, part, at:at + size] = jnp.broadcast_to(
                    value[first:first + size, None, :], (size, pairs, LANES))

    load_ext.wait()
    load_high.wait()
    load_low.wait()
    own = jnp.concatenate(
        [ext[HALF:HALF + rows, q * quarter:(q + 1) * quarter] for q in range(4)], axis=0)
    transform(0, own, 1.0, [(0, HALF, rows)])

    load_weight.wait()
    to_right.wait()
    to_left.wait()
    sides = [slice(0, HALF), slice(HALF + rows, 2 * HALF + rows)]
    edge = jnp.concatenate(
        [ext[side, q * quarter:(q + 1) * quarter] for q in range(4) for side in sides], axis=0)
    row = lax.broadcasted_iota(jnp.int32, (2 * HALF, LANES), 0)
    keep = jnp.where(row < HALF, (me > 0).astype(F32), (me < mids - 1).astype(F32))

    def beam_copy(c, k, to, source):
        return pltpu.make_async_remote_copy(
            send.at[c, to // rep],
            recv.at[c, pl.ds(pl.multiple_of(source * beams, beams), beams)],
            beam_send.at[c, k], beam_recv.at[c, source], device_id={"mid": to},
        )

    for c in range(chunks):
        if c > 0:
            transform(c, own, 1.0, [(0, HALF, rows)])
        transform(c, edge, keep, [(0, 0, HALF), (HALF, HALF + rows, HALF)])
        re = slice(c * LANES, (c + 1) * LANES)

        @pl.loop(0, beams)
        def _(b):
            centre = offset_ref[b] + HALF
            cos0 = weight[0, 0, :, re]
            a_re = cos0 * spec[c, 0, centre]
            a_im = cos0 * spec[c, 1, centre]
            b_re = jnp.zeros_like(a_re)
            b_im = jnp.zeros_like(a_re)
            for x in range(1, HALF + 1):
                r_up, r_dn = spec[c, 0, centre + x], spec[c, 0, centre - x]
                i_up, i_dn = spec[c, 1, centre + x], spec[c, 1, centre - x]
                cos, sin = weight[0, x, :, re], weight[1, x, :, re]
                a_re += cos * (r_up + r_dn)
                a_im += cos * (i_up + i_dn)
                b_re += sin * (i_up - i_dn)
                b_im += sin * (r_up - r_dn)
            at = pl.ds(pl.multiple_of(b * pairs, pairs), pairs)
            stage[c, 0, at, :] = a_re + b_re
            stage[c, 1, at, :] = a_im - b_im
            stage[c, 2, at, :] = a_re - b_re
            stage[c, 3, at, :] = a_im + b_im

        for p in range(pairs):
            for part in range(2):
                lanes = slice(part * LANES, (part + 1) * LANES)
                every = pl.ds(p, beams, stride=pairs)
                send[c, pairs + p, :, lanes] = stage.at[c, part][every, :].astype(BF16)
                send[c, pairs - 1 - p, :, lanes] = stage.at[c, 2 + part][every, :].astype(BF16)

        @pl.loop(0, mids - 1)
        def _(i):
            k = lax.rem(i + mids // 2, mids)
            k = jnp.where(i + mids // 2 >= mids, k + 1, k)
            beam_copy(c, k, lax.rem(me + k, mids), me).start()

        recv[c, pl.ds(pl.multiple_of(me * beams, beams), beams), :] = send[c, slope]

    lateral_first = lax.rem(me, rep) * laterals
    at_slope = lax.broadcasted_iota(jnp.int32, start_ref.shape, 0) == slope
    starts = jnp.sum(jnp.where(at_slope, start_ref[...], 0), axis=0, keepdims=True)
    beam_id = lax.broadcasted_iota(jnp.int32, (1, centres), 1)
    counts = jnp.zeros((1, centres), jnp.int32)
    for t in range(mids):
        inside = (beam_id >= t * beams) & (beam_id < (t + 1) * beams)
        counts = jnp.where(inside, count_ref[t] + t * beams, counts)
    target = jnp.where(beam_id < counts, starts + lateral_first, -1)
    hot = (target == lax.broadcasted_iota(jnp.int32, (centres, centres), 0)).astype(F32)
    hot = hot.astype(BF16)

    for load in load_oper:
        load.wait()

    for c in range(chunks):
        @pl.loop(1, mids)
        def _(k):
            beam_copy(c, k, lax.rem(me + k, mids), lax.rem(me + mids - k, mids)).wait()

        gathered = jnp.dot(hot, recv[c], preferred_element_type=F32).astype(BF16)
        held = jnp.zeros((centres, DEPTH), F32)
        for l in reversed(range(laterals)):
            foot = jnp.dot(
                gathered, oper[c, :, l * DEPTH:(l + 1) * DEPTH], preferred_element_type=F32)
            held = foot if l == laterals - 1 else pltpu.roll(held, 1, 0) + foot
        image[...] = held if c == 0 else image[...] + held

    outgoing[...] = image[...].astype(BF16)

    def part_copy(k, to, source):
        return pltpu.make_async_remote_copy(
            outgoing.at[pl.ds(pl.multiple_of(to * beams, beams), beams)], parts.at[source],
            part_send.at[k], part_recv.at[source], device_id={"mid": to},
        )

    @pl.loop(1, mids)
    def _(k):
        part_copy(k, lax.rem(me + k, mids), me).start()

    home = pl.ds(pl.multiple_of(me * beams, beams), beams)
    parts[me] = outgoing[home, :]

    @pl.loop(1, mids)
    def _(k):
        part_copy(k, lax.rem(me + k, mids), lax.rem(me + mids - k, mids)).wait()

    tile[...] = jnp.sum(parts[...].astype(F32), axis=0) * (1.0 / math.sqrt(FL * P_SIZE))

    def peer_copy(k, to, source):
        return pltpu.make_async_remote_copy(
            tile, peers.at[source], peer_send.at[k], peer_recv.at[source], device_id=to,
        )

    @pl.loop(1, group)
    def _(k):
        peer_copy(k, member(k)[1], mine).start()

    peers[mine] = tile[...]

    @pl.loop(1, group)
    def _(k):
        peer_copy(k, member(k)[1], lax.rem(mine + group - k, group)).wait()


def shards(traces, centre_offset, foot_start, beam_count, operator):
    mids, offs, subs = (lax.axis_size(name) for name in ("mid", "off", "sub"))
    traces = traces[0]
    if subs > 1:
        traces = lax.all_gather(traces, "sub", axis=1, tiled=True)
    rows, total = traces.shape
    samples, columns = operator.shape
    beams = centre_offset.shape[0]
    centres = foot_start.shape[0]
    group = offs * subs
    high, low = dft_quarter(total, subs)
    weight = half_weights(total, subs)
    pick = (lambda table: table[0]) if subs == 1 else (
        lambda table: lax.dynamic_index_in_dim(jnp.asarray(table), lax.axis_index("sub"), 0, False))
    high, low, weight = (jnp.asarray(pick(table)) for table in (high, low, weight))
    vmem = pl.BlockSpec(memory_space=pltpu.VMEM)
    smem = pl.BlockSpec(memory_space=pltpu.SMEM)
    hbm = pl.BlockSpec(memory_space=pltpu.HBM)
    dma = pltpu.SemaphoreType.DMA
    chunks = samples // 2 // LANES
    shares = pl.pallas_call(
        functools.partial(kernel, (mids, offs, subs)),
        out_shape=jax.ShapeDtypeStruct((group, beams, DEPTH), F32),
        in_specs=[hbm, smem, vmem, smem, hbm, hbm, hbm, hbm],
        out_specs=vmem,
        scratch_shapes=[
            pltpu.VMEM((rows + 2 * HALF, total), BF16),
            pltpu.VMEM(high.shape, BF16),
            pltpu.VMEM(low.shape, BF16),
            pltpu.VMEM(weight.shape, F32),
            pltpu.VMEM((chunks, 2 * LANES, columns), BF16),
            pltpu.VMEM((chunks, 2, rows + 2 * HALF, P_SIZE // 2, LANES), F32),
            pltpu.VMEM((chunks, 4, beams * P_SIZE // 2, LANES), F32),
            pltpu.VMEM((chunks, P_SIZE, beams, 2 * LANES), BF16),
            pltpu.VMEM((chunks, mids * beams, 2 * LANES), BF16),
            pltpu.VMEM((centres, DEPTH), F32),
            pltpu.VMEM((centres, DEPTH), BF16),
            pltpu.VMEM((mids, beams, DEPTH), BF16),
            pltpu.VMEM((beams, DEPTH), F32),
            dma((4,)),
            dma((chunks, 2)),
            dma((2,)),
            dma((2,)),
            dma((chunks, mids)),
            dma((chunks, mids)),
            dma((mids,)),
            dma((mids,)),
            dma((group,)),
            dma((group,)),
        ],
        compiler_params=pltpu.CompilerParams(
            collective_id=0, has_side_effects=True, vmem_limit_bytes=67043328),
    )(traces, centre_offset, foot_start.T, beam_count, operator, high, low, weight)
    return jnp.sum(shares, axis=0)


def solution(mesh):
    return jax.shard_map(
        shards,
        mesh=mesh,
        in_specs=(
            P("off", ("grp", "mid"), "sub"),
            P(("grp", "mid")),
            P("grp", None),
            P("grp"),
            P("sub", "mid"),
        ),
        out_specs=P(("grp", "mid"), None),
        check_vma=False,
    )
```
